32 devices in a mesh: batch: 8 (over z, y), seq: 4 (over x, core).
Axes of the slice: x: 2, y: 2, z: 4, core: 2. Of those that a mesh axis runs over, the one named last changes fastest.
Arguments:
- forward_embed: bfloat16 [12288, 1536], P(('batch', 'seq')), parts along dimension 0, may hold values from -6 to 6
- reverse_embed: bfloat16 [12288, 1536], P(('batch', 'seq')), parts along dimension 0, may hold values from -6 to 6
- conv_weight: bfloat16 [1, 3, 1536, 1536], P(None, None, 'seq'), may hold values from -0.09375 to 0.09375
- conv_bias: float32 [1, 1536], replicated, may hold values from -0.5 to 0.5
- head_weight: bfloat16 [1536, 1024], replicated, may hold values from -0.15625 to 0.15625
- head_bias: float32 [1024], replicated, may hold values from -1 to 1
Outputs:
- averaged: bfloat16 [12288, 1024], P(('batch', 'seq')), parts along dimension 0
The draws below stay inside these ranges and needn't reach their ends.
There are 8 independent parts, one for each index of `batch`. The reference program is written for one: setup_inputs(seed, part) draws one part's arguments, and reference() takes and returns one part's arrays. A program takes and returns all parts, laid end to end along the dimension named above; an argument that names none is the same for every part. Nothing has to cross between parts.
All inputs are finite; a program needn't handle non-finite values.
Results may differ from the reference program's by a relative error of at most 0.008.
Values may be sent and summed in bfloat16 or wider, within the bound.
A program may use at most 128 MiB of HBM per device.

```python
import jax
import jax.numpy as jnp

CHANNELS = 1536
TRACKS = 1024
LAYERS = 1
BINS = 1536


def level_of(stream_key, shape, cuts, low, high):
    level, own = 1.0, jax.random.fold_in(stream_key, 6)
    for dim, shards_of in cuts:
        heights = jnp.exp(jax.random.uniform(jax.random.fold_in(own, dim), (shards_of,), jnp.float32, low / len(cuts), high / len(cuts)))
        level = level * jnp.repeat(heights, shape[dim] // shards_of).reshape([-1 if axis == dim else 1 for axis in range(len(shape))])
    return level


def normal_values(key, extent, spread, limit, cuts=(), dtype=jnp.bfloat16):
    result = spread * jax.random.normal(key, extent, jnp.float32)
    if cuts:
        result = result * level_of(key, extent, cuts, -0.22, 0.18)
    return jnp.clip(result, -limit, limit).astype(dtype)


def setup_inputs(seed: int = 0, part: int = 0) -> dict:
    streams_of = jax.random.split(jax.random.key(seed), 7)
    own_keys = jax.random.split(jax.random.fold_in(streams_of[6], part), 7)
    forward_embed = normal_values(own_keys[0], (BINS, CHANNELS), 1.0, 6.0, ((0, 4),))
    reverse_embed = normal_values(own_keys[1], (BINS, CHANNELS), 1.0, 6.0, ((0, 4),))
    conv_weight = normal_values(streams_of[2], (LAYERS, 3, CHANNELS, CHANNELS), (3 * CHANNELS) ** -0.5, 0.09375, ((2, 4),))
    conv_bias = jnp.clip(jax.random.uniform(streams_of[3], (LAYERS, CHANNELS), jnp.float32, -0.5, 0.5), -0.5, 0.5)
    head_weight = normal_values(streams_of[4], (CHANNELS, TRACKS), CHANNELS ** -0.5, 0.15625)
    head_bias = jnp.clip(jax.random.uniform(streams_of[5], (TRACKS,), jnp.float32, -1.0, 1.0), -1.0, 1.0)
    return dict(forward_embed=forward_embed, reverse_embed=reverse_embed, conv_weight=conv_weight, conv_bias=conv_bias, head_weight=head_weight, head_bias=head_bias)


def convolve(hidden, kernel, bias):
    count = hidden.shape[0]
    padded = jnp.pad(hidden, ((1, 1), (0, 0)))
    acc = jnp.zeros((count, kernel.shape[2]), jnp.float32)
    for tap in range(3):
        acc = acc + jnp.dot(padded[tap:tap + count], kernel[tap], preferred_element_type=jnp.float32)
    return jax.nn.gelu(acc + bias, approximate=False).astype(jnp.bfloat16)


def strand_tracks(embed, conv_weight, conv_bias, head_weight, head_bias):
    hidden = embed
    for layer in range(LAYERS):
        hidden = convolve(hidden, conv_weight[layer], conv_bias[layer])
    logits = jnp.dot(hidden, head_weight, preferred_element_type=jnp.float32) + head_bias
    return jax.nn.softplus(logits).astype(jnp.bfloat16)


def reference(forward_embed, reverse_embed, conv_weight, conv_bias, head_weight, head_bias):
    forward_tracks = strand_tracks(forward_embed, conv_weight, conv_bias, head_weight, head_bias)
    reverse_tracks = strand_tracks(reverse_embed, conv_weight, conv_bias, head_weight, head_bias)
    mean = 0.5 * (forward_tracks.astype(jnp.float32) + reverse_tracks[::-1].astype(jnp.float32))
    return mean.astype(jnp.bfloat16)
```

```python
import functools
import math

import jax
import jax.numpy as jnp
from jax import lax
from jax.experimental import pallas as pl
from jax.experimental.pallas import tpu as pltpu
from jax.sharding import PartitionSpec as P

MESH = pl.DeviceIdType.MESH
F32 = jnp.float32
BF16 = jnp.bfloat16
UNIT = 128


def gelu(x):
    return (0.5 * x) * (1.0 + lax.erf(x * math.sqrt(0.5)))


def softplus(x):
    u = jnp.exp(-jnp.abs(x))
    return jnp.maximum(x, 0.0) + jnp.where(u < 1e-3, u - 0.5 * u * u, jnp.log(1.0 + u))


def kernel(
    taps, fwd_hbm, rev_hbm, w_hbm, cb_ref, hw_hbm, hb_ref, out_ref,
    embed, halo, xcat, wbuf, acc, headw, logits, flip, sendt, recvt,
    local_sem, halo_send, halo_recv, own_send, own_recv,
    x_send, x_recv, y_send, y_recv, z_send, z_recv, m_send, m_recv, t_send, t_recv,
):
    s = lax.axis_index("seq")
    b = lax.axis_index("batch")
    core = s % 2
    far = s // 2
    mate = s + 1 - 2 * core
    across = s + 2 - 4 * far
    mirror = 3 - s
    shards = (s, mate, across, mirror)
    y = b % 2
    z = (b // 2) % 2
    yp = b + 1 - 2 * y
    zp = b + 2 - 4 * z
    cx = y + (1 - y) * 2 * z
    cy = (1 - y) + y * 2 * z
    cz = 2 * (1 - z)
    rows, channels = embed.shape[1:]
    depth = w_hbm.shape[2]
    units = channels // UNIT
    wide = 2 * UNIT
    blocks = channels // wide
    half = 2 * taps * depth
    tracks = hb_ref.shape[1]
    pieces = tracks // wide

    barrier = pltpu.get_barrier_semaphore()
    for peer in ({"seq": mate}, {"seq": across}, {"seq": mirror}, {"batch": yp}, {"batch": zp}):
        pl.semaphore_signal(barrier, inc=1, device_id=peer, device_id_type=MESH)

    loads = [
        pltpu.make_async_copy(fwd_hbm, embed.at[0], local_sem.at[0]),
        pltpu.make_async_copy(rev_hbm, embed.at[1], local_sem.at[1]),
        pltpu.make_async_copy(hw_hbm, headw, local_sem.at[2]),
    ] + [
        pltpu.make_async_copy(w_hbm.at[0, k], wbuf.at[pl.ds(k * depth, depth)], local_sem.at[3 + k])
        for k in range(taps)
    ]
    for copy in loads:
        copy.start()
    pl.semaphore_wait(barrier, 5)

    def remote(src, dst, send, recv, peer):
        return pltpu.make_async_remote_copy(
            src_ref=src, dst_ref=dst, send_sem=send, recv_sem=recv, device_id=peer, device_id_type=MESH
        )

    tile = halo.shape[2]
    halos = []
    for k, src in enumerate((fwd_hbm, rev_hbm)):
        halos.append(remote(src.at[pl.ds(rows - tile, tile)], halo.at[k, 0], halo_send.at[k, 0], halo_recv.at[k, 0], {"seq": (s + 1) % 4}))
        halos.append(remote(src.at[pl.ds(0, tile)], halo.at[k, 1], halo_send.at[k, 1], halo_recv.at[k, 1], {"seq": (s + 3) % 4}))
    for copy in halos:
        copy.start()

    def cell(slot, tap, unit):
        row = pl.multiple_of((slot * taps + tap) * depth, depth)
        return wbuf.at[pl.ds(row, depth), pl.ds(pl.multiple_of(unit * UNIT, UNIT), UNIT)]

    def x_copy(j):
        src = w_hbm.at[0, cx, :, pl.ds(pl.multiple_of(j * UNIT, UNIT), UNIT)]
        return remote(src, cell(2, cx, j), x_send.at[j], x_recv.at[j], {"seq": across})

    def y_copy(color, j):
        return remote(cell(2, color, j), cell(2, color, j), y_send.at[j], y_recv.at[j], {"batch": yp})

    def z_copy(color, j):
        return remote(cell(2, color, j), cell(2, color, j), z_send.at[j], z_recv.at[j], {"batch": zp})

    def m_copy(kind, color, j):
        return remote(cell(2, color, j), cell(3, color, j), m_send.at[kind, j], m_recv.at[kind, j], {"seq": mate})

    own = [
        remote(w_hbm.at[0, k], wbuf.at[pl.ds((taps + k) * depth, depth)], own_send.at[k], own_recv.at[k], {"seq": mate})
        for k in range(taps)
    ]

    def start_x(j, c):
        x_copy(j).start()
        return c

    lax.fori_loop(0, units, start_x, 0)
    for copy in own:
        copy.start()

    r = lax.broadcasted_iota(jnp.int32, (rows, rows), 0)
    c = lax.broadcasted_iota(jnp.int32, (rows, rows), 1)
    flip[...] = jnp.where(r + c == rows - 1, 1.0, 0.0).astype(BF16)

    for copy in loads[:2]:
        copy.wait()
    for copy in halos:
        copy.wait()
    line = lax.broadcasted_iota(jnp.int32, (rows, depth), 0)
    for k in range(2):
        for slot in range(4):
            cols = pl.ds(pl.multiple_of(shards[slot] * depth, UNIT), depth)
            mid = embed[k, :, cols]
            wide_mid = mid.astype(F32)
            low = halo[k, 0, :, cols].astype(F32)[tile - 1 : tile]
            high = halo[k, 1, :, cols].astype(F32)[0:1]
            low = jnp.where(s == 0, 0.0, low)
            high = jnp.where(s == 3, 0.0, high)
            before = jnp.where(line == 0, low, pltpu.roll(wide_mid, 1, 0))
            after = jnp.where(line == rows - 1, high, pltpu.roll(wide_mid, rows - 1, 0))
            for tap, part in enumerate((before.astype(BF16), mid, after.astype(BF16))):
                xcat[k, :, pl.ds((slot * taps + tap) * depth, depth)] = part

    def near(m):
        cols = pl.ds(pl.multiple_of(m * wide, wide), wide)
        w = wbuf[pl.ds(0, half), cols]
        for k in range(2):
            acc[k, :, cols] = jnp.dot(xcat[k, :, pl.ds(0, half)], w, preferred_element_type=F32) + cb_ref[:, cols]

    def remote_part(k, m):
        cols = pl.ds(pl.multiple_of(m * wide, wide), wide)
        total = acc[k, :, cols] + jnp.dot(
            xcat[k, :, pl.ds(half, half)], wbuf[pl.ds(half, half), cols], preferred_element_type=F32
        )
        hidden = gelu(total).astype(BF16)
        logits[k] = logits[k] + jnp.dot(hidden, headw[cols, :], preferred_element_type=F32)

    for copy in loads[2:]:
        copy.wait()
    for copy in own:
        copy.wait()
    for k in range(2):
        logits[k] = jnp.broadcast_to(hb_ref[...], (rows, tracks))
    lead = 2

    def first(m, carry):
        near(m)
        return carry

    lax.fori_loop(0, lead, first, 0)

    def step(j, carry):
        @pl.when(j < units)
        def _():
            x_copy(j).wait_recv()
            y_copy(cx, j).start()

            @pl.when(y == 0)
            def _():
                z_copy(cx, j).start()

            m_copy(0, cx, j).start()

        @pl.when((j >= 1) & (j < units + 1))
        def _():
            y_copy(cy, j - 1).wait_recv()

            @pl.when(y == 1)
            def _():
                z_copy(cy, j - 1).start()

            m_copy(1, cy, j - 1).start()

        @pl.when((j >= 2) & (j < units + 2))
        def _():
            z_copy(cz, j - 2).wait_recv()
            m_copy(2, cz, j - 2).start()

        @pl.when(j < blocks - lead)
        def _():
            near(j + lead)

        @pl.when(j >= 4)
        def _():
            k = (j + 1) % 2
            m = (j - 4) // 2

            @pl.when(k == 1)
            def _():
                for kind, color in enumerate((cx, cy, cz)):
                    m_copy(kind, color, 2 * m).wait_recv()
                    m_copy(kind, color, 2 * m + 1).wait_recv()

            remote_part(k, m)

        return carry

    lax.fori_loop(0, 2 * blocks + 3, step, 0)

    def t_copy(p):
        cols = pl.ds(p * wide, wide)
        return remote(sendt.at[:, cols], recvt.at[:, cols], t_send.at[p], t_recv.at[p], {"seq": mirror})

    for p in range(pieces):
        cols = pl.ds(p * wide, wide)
        value = softplus(logits[1, :, cols]).astype(BF16)
        sendt[:, cols] = jnp.dot(flip[...], value, preferred_element_type=F32).astype(BF16)
        if p:
            t_copy(p - 1).start()
    remote_part(0, blocks - 1)
    t_copy(pieces - 1).start()
    for p in range(pieces):
        cols = pl.ds(p * wide, wide)
        logits[0, :, cols] = softplus(logits[0, :, cols]).astype(BF16).astype(F32)
    for p in range(pieces):
        cols = pl.ds(p * wide, wide)
        t_copy(p).wait_recv()
        out_ref[:, cols] = (0.5 * (logits[0, :, cols] + recvt[:, cols].astype(F32))).astype(BF16)

    def drain(j, carry):
        x_copy(j).wait_send()
        y_copy(cx, j).wait_send()
        z_copy(2 * z, j).wait_send()
        for kind, color in enumerate((cx, cy, cz)):
            m_copy(kind, color, j).wait_send()
        return carry

    lax.fori_loop(0, units, drain, 0)
    for p in range(pieces):
        t_copy(p).wait_send()


def fused(forward_embed, reverse_embed, conv_weight, conv_bias, head_weight, head_bias):
    rows, channels = forward_embed.shape
    _, taps, depth, _ = conv_weight.shape
    tracks = head_weight.shape[1]
    units = channels // UNIT
    pieces = tracks // (2 * UNIT)
    dma = pltpu.SemaphoreType.DMA
    anywhere = pl.BlockSpec(memory_space=pl.ANY)
    vmem = pl.BlockSpec(memory_space=pltpu.VMEM)
    return pl.pallas_call(
        functools.partial(kernel, taps),
        out_shape=jax.ShapeDtypeStruct((rows, tracks), BF16),
        in_specs=[anywhere, anywhere, anywhere, vmem, anywhere, vmem],
        out_specs=vmem,
        scratch_shapes=[
            pltpu.VMEM((2, rows, channels), BF16),
            pltpu.VMEM((2, 2, 16, channels), BF16),
            pltpu.VMEM((2, rows, 4 * taps * depth), BF16),
            pltpu.VMEM((4 * taps * depth, channels), BF16),
            pltpu.VMEM((2, rows, channels), F32),
            pltpu.VMEM((channels, tracks), BF16),
            pltpu.VMEM((2, rows, tracks), F32),
            pltpu.VMEM((rows, rows), BF16),
            pltpu.VMEM((rows, tracks), BF16),
            pltpu.VMEM((rows, tracks), BF16),
            dma((3 + taps,)),
            dma((2, 2)), dma((2, 2)),
            dma((taps,)), dma((taps,)),
            dma((units,)), dma((units,)),
            dma((units,)), dma((units,)),
            dma((units,)), dma((units,)),
            dma((3, units)), dma((3, units)),
            dma((pieces,)), dma((pieces,)),
        ],
        compiler_params=pltpu.CompilerParams(
            collective_id=0, has_side_effects=True, vmem_limit_bytes=62 * 1024 * 1024
        ),
    )(forward_embed, reverse_embed, conv_weight, conv_bias, head_weight, head_bias[None])


def with_halo(block, axis):
    count = lax.axis_size(axis)
    forward = [(i, i + 1) for i in range(count - 1)]
    backward = [(target, source) for source, target in forward]
    low = lax.ppermute(block[-1:], axis, forward)
    high = lax.ppermute(block[:1], axis, backward)
    return jnp.concatenate([low, block, high], axis=0)


def general(forward_embed, reverse_embed, conv_weight, conv_bias, head_weight, head_bias):
    count = lax.axis_size("seq")
    layers, taps = conv_weight.shape[:2]
    gathered = [lax.all_gather(conv_weight[n], "seq", axis=1, tiled=True) for n in range(layers)]

    def strand(hidden):
        for n in range(layers):
            rows = hidden.shape[0]
            padded = with_halo(hidden, "seq")
            total = sum(
                jnp.dot(padded[k : k + rows], gathered[n][k], preferred_element_type=F32) for k in range(taps)
            )
            hidden = jax.nn.gelu(total + conv_bias[n], approximate=False).astype(BF16)
        logits = jnp.dot(hidden, head_weight, preferred_element_type=F32) + head_bias
        return jax.nn.softplus(logits).astype(BF16)

    reverse_tracks = strand(reverse_embed)[::-1]
    reverse_tracks = lax.ppermute(reverse_tracks, "seq", [(i, count - 1 - i) for i in range(count)])
    mean = 0.5 * (strand(forward_embed).astype(F32) + reverse_tracks.astype(F32))
    return mean.astype(BF16)


def solution(mesh):
    cubes = mesh.shape["seq"] == 4 and mesh.shape["batch"] % 4 == 0
    return jax.shard_map(
        fused if cubes else general,
        mesh=mesh,
        in_specs=(
            P(("batch", "seq"), None),
            P(("batch", "seq"), None),
            P(None, None, "seq", None),
            P(),
            P(),
            P(),
        ),
        out_specs=P(("batch", "seq"), None),
        check_vma=False,
    )
```

```python
import functools
import math

import jax
import jax.numpy as jnp
from jax import lax
from jax.experimental import pallas as pl
from jax.experimental.pallas import tpu as pltpu
from jax.sharding import PartitionSpec as P

MESH = pl.DeviceIdType.MESH
F32 = jnp.float32
BF16 = jnp.bfloat16
LANES = 128
WIDE = 256
SPLIT = 2
LAG = 2


def gelu(x):
    return (0.5 * x) * (1.0 + lax.erf(x * math.sqrt(0.5)))


def softplus(x):
    u = jnp.exp(-jnp.abs(x))
    return jnp.maximum(x, 0.0) + jnp.where(u < 1e-3, u - 0.5 * u * u, jnp.log(1.0 + u))


def kernel(
    taps, fwd_hbm, rev_hbm, w_hbm, cb_ref, hw_hbm, hb_ref, fwd_out, rev_out,
    embed, halo, xcat, wbuf, acc, headw, logits, flip, sendt, keept,
    local_sem, halo_send, halo_recv, own_send, own_recv,
    x_send, x_recv, y_send, y_recv, z_send, z_recv, m_send, m_recv, t_send, t_recv, out_sem,
):
    s = lax.axis_index("seq")
    b = lax.axis_index("batch")
    core = s % 2
    far = s // 2
    mate = s + 1 - 2 * core
    across = s + 2 - 4 * far
    mirror = 3 - s
    shards = (s, mate, across, mirror)
    y = b % 2
    z = (b // 2) % 2
    yp = b + 1 - 2 * y
    zp = b + 2 - 4 * z
    cx = y + (1 - y) * 2 * z
    cy = (1 - y) + y * 2 * z
    cz = 2 * (1 - z)
    rows, channels = embed.shape[1:]
    depth = w_hbm.shape[2]
    wide = WIDE
    blocks = channels // wide
    units = SPLIT * blocks
    part = depth // SPLIT
    half = 2 * taps * depth
    tracks = hb_ref.shape[1]
    pieces = tracks // wide

    barrier = pltpu.get_barrier_semaphore()
    for peer in ({"seq": mate}, {"seq": across}, {"seq": mirror}, {"batch": yp}, {"batch": zp}):
        pl.semaphore_signal(barrier, inc=1, device_id=peer, device_id_type=MESH)

    loads = [
        pltpu.make_async_copy(fwd_hbm, embed.at[0], local_sem.at[0]),
        pltpu.make_async_copy(rev_hbm, embed.at[1], local_sem.at[1]),
        pltpu.make_async_copy(hw_hbm, headw, local_sem.at[2]),
    ] + [
        pltpu.make_async_copy(
            w_hbm.at[0, k, :, pl.ds(m * wide, wide)], wbuf.at[m, pl.ds(k * depth, depth)], local_sem.at[3 + k * blocks + m]
        )
        for m in range(blocks)
        for k in range(taps)
    ]
    for copy in loads:
        copy.start()
    pl.semaphore_wait(barrier, 5)

    def remote(src, dst, send, recv, peer):
        return pltpu.make_async_remote_copy(
            src_ref=src, dst_ref=dst, send_sem=send, recv_sem=recv, device_id=peer, device_id_type=MESH
        )

    tile = halo.shape[2]
    halos = []
    for k, src in enumerate((fwd_hbm, rev_hbm)):
        halos.append(remote(src.at[pl.ds(rows - tile, tile)], halo.at[k, 0], halo_send.at[k, 0], halo_recv.at[k, 0], {"seq": (s + 1) % 4}))
        halos.append(remote(src.at[pl.ds(0, tile)], halo.at[k, 1], halo_send.at[k, 1], halo_recv.at[k, 1], {"seq": (s + 3) % 4}))
    for copy in halos:
        copy.start()

    def cell(slot, tap, unit):
        row = pl.multiple_of((slot * taps + tap) * depth + (unit % SPLIT) * part, 32)
        return wbuf.at[unit // SPLIT, pl.ds(row, part)]

    def x_copy(j):
        row = pl.ds(pl.multiple_of((j % SPLIT) * part, 32), part)
        col = pl.ds(pl.multiple_of((j // SPLIT) * wide, wide), wide)
        return remote(w_hbm.at[0, cx, row, col], cell(2, cx, j), x_send.at[j], x_recv.at[j], {"seq": across})

    def y_copy(color, j):
        return remote(cell(2, color, j), cell(2, color, j), y_send.at[j], y_recv.at[j], {"batch": yp})

    def z_copy(color, j):
        return remote(cell(2, color, j), cell(2, color, j), z_send.at[j], z_recv.at[j], {"batch": zp})

    def m_copy(kind, color, j):
        return remote(cell(2, color, j), cell(3, color, j), m_send.at[kind, j], m_recv.at[kind, j], {"seq": mate})

    own = [
        remote(
            w_hbm.at[0, k, :, pl.ds(m * wide, wide)], wbuf.at[m, pl.ds((taps + k) * depth, depth)],
            own_send.at[k, m], own_recv.at[k, m], {"seq": mate},
        )
        for m in range(blocks)
        for k in range(taps)
    ]

    def start_x(j, c):
        x_copy(j).start()
        return c

    lax.fori_loop(0, units, start_x, 0)
    for copy in own:
        copy.start()

    r = lax.broadcasted_iota(jnp.int32, (rows, rows), 0)
    c = lax.broadcasted_iota(jnp.int32, (rows, rows), 1)
    flip[...] = jnp.where(r + c == rows - 1, 1.0, 0.0).astype(BF16)
    for k in range(2):
        logits[k] = jnp.broadcast_to(hb_ref[...], (rows, tracks))

    line = lax.broadcasted_iota(jnp.int32, (rows, depth), 0)

    def build(k, slot):
        shard = (s // 2 + (slot // 2) * (1 - 2 * far)) * 2 + core + (slot % 2) * (1 - 2 * core)
        cols = pl.ds(pl.multiple_of(shard * depth, LANES), depth)
        mid = embed[k, :, cols]
        wide_mid = mid.astype(F32)
        low = halo[k, 0, :, cols].astype(F32)[tile - 1 : tile]
        high = halo[k, 1, :, cols].astype(F32)[0:1]
        low = jnp.where(s == 0, 0.0, low)
        high = jnp.where(s == 3, 0.0, high)
        before = jnp.where(line == 0, low, pltpu.roll(wide_mid, 1, 0))
        after = jnp.where(line == rows - 1, high, pltpu.roll(wide_mid, rows - 1, 0))
        for tap, value in enumerate((before.astype(BF16), mid, after.astype(BF16))):
            xcat[k, :, pl.ds(pl.multiple_of((slot * taps + tap) * depth, LANES), depth)] = value

    def near(k, m):
        cols = pl.ds(pl.multiple_of(m * wide, wide), wide)
        acc[k, :, cols] = (
            jnp.dot(xcat[k, :, pl.ds(0, half)], wbuf[m, pl.ds(0, half)], preferred_element_type=F32)
            + cb_ref[:, cols]
        )

    def remote_part(k, m):
        cols = pl.ds(pl.multiple_of(m * wide, wide), wide)
        total = acc[k, :, cols] + jnp.dot(
            xcat[k, :, pl.ds(half, half)], wbuf[m, pl.ds(half, half)], preferred_element_type=F32
        )
        hidden = gelu(total).astype(BF16)
        logits[k] = logits[k] + jnp.dot(hidden, headw[cols, :], preferred_element_type=F32)

    for copy in loads[:2]:
        copy.wait()
    for copy in halos:
        copy.wait()

    def first(i, carry):
        build(i % 2, i // 2)
        return carry

    lax.fori_loop(0, 4, first, 0)

    def step(j, carry):
        @pl.when(j < units)
        def _():
            x_copy(j).wait_recv()
            y_copy(cx, j).start()

            @pl.when(y == 0)
            def _():
                z_copy(cx, j).start()

            m_copy(0, cx, j).start()

        @pl.when((j >= LAG) & (j < units + LAG))
        def _():
            y_copy(cy, j - LAG).wait_recv()

            @pl.when(y == 1)
            def _():
                z_copy(cy, j - LAG).start()

            m_copy(1, cy, j - LAG).start()

        @pl.when((j >= 2 * LAG) & (j < units + 2 * LAG))
        def _():
            z_copy(cz, j - 2 * LAG).wait_recv()
            m_copy(2, cz, j - 2 * LAG).start()

        @pl.when(j == 0)
        def _():
            lax.fori_loop(4, 8, first, 0)
            for copy in loads[2:]:
                copy.wait()
            for copy in own:
                copy.wait()

        pace = SPLIT // 2

        @pl.when((j >= 1) & ((j - 1) % pace == 0) & (j < units + 1))
        def _():
            i = (j - 1) // pace
            near(1 - i % 2, i // 2)

        late = j - SPLIT - 2 * LAG

        @pl.when((late >= 0) & (late % pace == 0))
        def _():
            k = 1 - late // pace % 2
            m = late // SPLIT

            @pl.when(k == 1)
            def _():
                for kind, color in enumerate((cx, cy, cz)):
                    for u in range(SPLIT):
                        m_copy(kind, color, SPLIT * m + u).wait_recv()

            remote_part(k, m)

        return carry

    lax.fori_loop(0, units + 2 * LAG + 1, step, 0)

    def t_copy(p):
        cols = pl.ds(p * wide, wide)
        return remote(sendt.at[:, cols], rev_out.at[:, cols], t_send.at[p], t_recv.at[p], {"seq": mirror})

    for p in range(pieces):
        cols = pl.ds(p * wide, wide)
        value = softplus(logits[1, :, cols]).astype(BF16)
        sendt[:, cols] = jnp.dot(flip[...], value, preferred_element_type=F32).astype(BF16)
        if p:
            t_copy(p - 1).start()
    remote_part(0, blocks - 1)
    t_copy(pieces - 1).start()
    keep = []
    for p in range(pieces):
        cols = pl.ds(p * wide, wide)
        keept[:, cols] = softplus(logits[0, :, cols]).astype(BF16)
        keep.append(pltpu.make_async_copy(keept.at[:, cols], fwd_out.at[:, cols], out_sem.at[p]))
        if p:
            keep[p - 1].start()

    def drain(j, carry):
        x_copy(j).wait_send()
        y_copy(cx, j).wait_send()
        z_copy(2 * z, j).wait_send()
        for kind, color in enumerate((cx, cy, cz)):
            m_copy(kind, color, j).wait_send()
        return carry

    lax.fori_loop(0, units, drain, 0)
    keep[-1].start()
    for copy in keep:
        copy.wait()
    for p in range(pieces):
        t_copy(p).wait()


def fused(forward_embed, reverse_embed, conv_weight, conv_bias, head_weight, head_bias):
    rows, channels = forward_embed.shape
    _, taps, depth, _ = conv_weight.shape
    tracks = head_weight.shape[1]
    blocks = channels // WIDE
    units = SPLIT * blocks
    pieces = tracks // WIDE
    dma = pltpu.SemaphoreType.DMA
    anywhere = pl.BlockSpec(memory_space=pl.ANY)
    vmem = pl.BlockSpec(memory_space=pltpu.VMEM)
    forward_tracks, reverse_tracks = pl.pallas_call(
        functools.partial(kernel, taps),
        out_shape=[jax.ShapeDtypeStruct((rows, tracks), BF16)] * 2,
        in_specs=[anywhere, anywhere, anywhere, vmem, anywhere, vmem],
        out_specs=[anywhere, anywhere],
        scratch_shapes=[
            pltpu.VMEM((2, rows, channels), BF16),
            pltpu.VMEM((2, 2, 16, channels), BF16),
            pltpu.VMEM((2, rows, 4 * taps * depth), BF16),
            pltpu.VMEM((blocks, 4 * taps * depth, WIDE), BF16),
            pltpu.VMEM((2, rows, channels), F32),
            pltpu.VMEM((channels, tracks), BF16),
            pltpu.VMEM((2, rows, tracks), F32),
            pltpu.VMEM((rows, rows), BF16),
            pltpu.VMEM((rows, tracks), BF16),
            pltpu.VMEM((rows, tracks), BF16),
            dma((3 + taps * blocks,)),
            dma((2, 2)), dma((2, 2)),
            dma((taps, blocks)), dma((taps, blocks)),
            dma((units,)), dma((units,)),
            dma((units,)), dma((units,)),
            dma((units,)), dma((units,)),
            dma((3, units)), dma((3, units)),
            dma((pieces,)), dma((pieces,)), dma((pieces,)),
        ],
        compiler_params=pltpu.CompilerParams(
            collective_id=0, has_side_effects=True, vmem_limit_bytes=62 * 1024 * 1024
        ),
    )(forward_embed, reverse_embed, conv_weight, conv_bias, head_weight, head_bias[None])
    return (0.5 * (forward_tracks.astype(F32) + reverse_tracks.astype(F32))).astype(BF16)


def with_halo(block, axis):
    count = lax.axis_size(axis)
    forward = [(i, i + 1) for i in range(count - 1)]
    backward = [(target, source) for source, target in forward]
    low = lax.ppermute(block[-1:], axis, forward)
    high = lax.ppermute(block[:1], axis, backward)
    return jnp.concatenate([low, block, high], axis=0)


def general(forward_embed, reverse_embed, conv_weight, conv_bias, head_weight, head_bias):
    count = lax.axis_size("seq")
    layers, taps = conv_weight.shape[:2]
    gathered = [lax.all_gather(conv_weight[n], "seq", axis=1, tiled=True) for n in range(layers)]

    def strand(hidden):
        for n in range(layers):
            rows = hidden.shape[0]
            padded = with_halo(hidden, "seq")
            total = sum(
                jnp.dot(padded[k : k + rows], gathered[n][k], preferred_element_type=F32) for k in range(taps)
            )
            hidden = jax.nn.gelu(total + conv_bias[n], approximate=False).astype(BF16)
        logits = jnp.dot(hidden, head_weight, preferred_element_type=F32) + head_bias
        return jax.nn.softplus(logits).astype(BF16)

    reverse_tracks = strand(reverse_embed)[::-1]
    reverse_tracks = lax.ppermute(reverse_tracks, "seq", [(i, count - 1 - i) for i in range(count)])
    mean = 0.5 * (strand(forward_embed).astype(F32) + reverse_tracks.astype(F32))
    return mean.astype(BF16)


def solution(mesh):
    cubes = mesh.shape["seq"] == 4 and mesh.shape["batch"] % 4 == 0
    return jax.shard_map(
        fused if cubes else general,
        mesh=mesh,
        in_specs=(
            P(("batch", "seq"), None),
            P(("batch", "seq"), None),
            P(None, None, "seq", None),
            P(),
            P(),
            P(),
        ),
        out_specs=P(("batch", "seq"), None),
        check_vma=False,
    )
```

```python
import functools
import math

import jax
import jax.numpy as jnp
from jax import lax
from jax.experimental import pallas as pl
from jax.experimental.pallas import tpu as pltpu
from jax.sharding import PartitionSpec as P

MESH = pl.DeviceIdType.MESH
F32 = jnp.float32
BF16 = jnp.bfloat16
LANES = 128
WIDE = 256
SPLIT = 2
LAG = 2


def gelu(x):
    return (0.5 * x) * (1.0 + lax.erf(x * math.sqrt(0.5)))


def softplus(x):
    u = jnp.exp(-jnp.abs(x))
    return jnp.maximum(x, 0.0) + jnp.where(u < 1e-3, u - 0.5 * u * u, jnp.log(1.0 + u))


def kernel(
    taps, fwd_hbm, rev_hbm, w_hbm, cb_ref, hw_hbm, hb_ref, fwd_out, rev_out,
    embed, halo, guest, xcat, wbuf, acc, headw, logits, flip, sendt, keept,
    local_sem, halo_send, halo_recv, own_send, own_recv,
    x_send, x_recv, y_send, y_recv, z_send, z_recv, m_send, m_recv, t_send, t_recv, out_sem, guest_sem,
):
    s = lax.axis_index("seq")
    b = lax.axis_index("batch")
    core = s % 2
    far = s // 2
    mate = s + 1 - 2 * core
    across = s + 2 - 4 * far
    mirror = 3 - s
    shards = (s, mate, across, mirror)
    y = b % 2
    z = (b // 2) % 2
    yp = b + 1 - 2 * y
    zp = b + 2 - 4 * z
    cx = y + (1 - y) * 2 * z
    cy = (1 - y) + y * 2 * z
    cz = 2 * (1 - z)
    rows, channels = embed.shape[1:]
    depth = w_hbm.shape[2]
    wide = WIDE
    blocks = channels // wide
    units = SPLIT * blocks
    part = depth // SPLIT
    half = 2 * taps * depth
    tracks = hb_ref.shape[1]
    pieces = tracks // wide
    visit = guest.shape[0] - halo.shape[2]
    kept = rows - visit

    barrier = pltpu.get_barrier_semaphore()
    for peer in ({"seq": mate}, {"seq": across}, {"seq": mirror}, {"batch": yp}, {"batch": zp}):
        pl.semaphore_signal(barrier, inc=1, device_id=peer, device_id_type=MESH)

    loads = [
        pltpu.make_async_copy(fwd_hbm, embed.at[0], local_sem.at[0]),
        pltpu.make_async_copy(rev_hbm, embed.at[1], local_sem.at[1]),
        pltpu.make_async_copy(hw_hbm, headw, local_sem.at[2]),
    ] + [
        pltpu.make_async_copy(
            w_hbm.at[0, k, :, pl.ds(m * wide, wide)], wbuf.at[m, pl.ds(k * depth, depth)], local_sem.at[3 + k * blocks + m]
        )
        for m in range(blocks)
        for k in range(taps)
    ]
    for copy in loads:
        copy.start()
    pl.semaphore_wait(barrier, 5)

    def remote(src, dst, send, recv, peer):
        return pltpu.make_async_remote_copy(
            src_ref=src, dst_ref=dst, send_sem=send, recv_sem=recv, device_id=peer, device_id_type=MESH
        )

    tile = halo.shape[2]
    halos = []
    for k, src in enumerate((fwd_hbm, rev_hbm)):
        halos.append(remote(src.at[pl.ds(rows - tile, tile)], halo.at[k, 0], halo_send.at[k, 0], halo_recv.at[k, 0], {"seq": (s + 1) % 4}))
        target = (s + 3) % 4 if k == 0 else across
        halos.append(remote(src.at[pl.ds(0, tile)], halo.at[k, 1], halo_send.at[k, 1], halo_recv.at[k, 1], {"seq": target}))
    for copy in halos:
        copy.start()

    def cell(slot, tap, unit):
        row = pl.multiple_of((slot * taps + tap) * depth + (unit % SPLIT) * part, 32)
        return wbuf.at[unit // SPLIT, pl.ds(row, part)]

    def x_copy(j):
        row = pl.ds(pl.multiple_of((j % SPLIT) * part, 32), part)
        col = pl.ds(pl.multiple_of((j // SPLIT) * wide, wide), wide)
        return remote(w_hbm.at[0, cx, row, col], cell(2, cx, j), x_send.at[j], x_recv.at[j], {"seq": across})

    def y_copy(color, j):
        return remote(cell(2, color, j), cell(2, color, j), y_send.at[j], y_recv.at[j], {"batch": yp})

    def z_copy(color, j):
        return remote(cell(2, color, j), cell(2, color, j), z_send.at[j], z_recv.at[j], {"batch": zp})

    def m_copy(kind, color, j):
        return remote(cell(2, color, j), cell(3, color, j), m_send.at[kind, j], m_recv.at[kind, j], {"seq": mate})

    guests = remote(
        rev_hbm.at[pl.ds(kept - tile, visit + tile)], guest, guest_sem.at[0], guest_sem.at[1], {"seq": mirror}
    )
    own = [
        remote(
            w_hbm.at[0, k, :, pl.ds(m * wide, wide)], wbuf.at[m, pl.ds((taps + k) * depth, depth)],
            own_send.at[k, m], own_recv.at[k, m], {"seq": mate},
        )
        for m in range(blocks)
        for k in range(taps)
    ]

    def start_x(j, c):
        x_copy(j).start()
        return c

    lax.fori_loop(0, units, start_x, 0)
    for copy in own:
        copy.start()

    r = lax.broadcasted_iota(jnp.int32, (rows, rows), 0)
    c = lax.broadcasted_iota(jnp.int32, (rows, rows), 1)
    flip[...] = jnp.where(r + c == rows - 1, 1.0, 0.0).astype(BF16)
    for k in range(2):
        logits[k] = jnp.broadcast_to(hb_ref[...], (rows, tracks))

    line = lax.broadcasted_iota(jnp.int32, (rows, depth), 0)

    def shard_of(slot):
        return (far + (slot // 2) * (1 - 2 * far)) * 2 + core + (slot % 2) * (1 - 2 * core)

    def build_guest(slot, carry):
        cols = pl.ds(pl.multiple_of(shard_of(slot) * depth, LANES), depth)
        full = guest[:, cols].astype(F32)
        high = jnp.where(s == 2, embed[1, pl.ds(0, tile), cols], halo[1, 1, :, cols]).astype(F32)[0:1]
        high = jnp.where(s == 0, 0.0, high)
        before = pltpu.roll(full, 1, 0)[tile:]
        after = pltpu.roll(full, visit + tile - 1, 0)[tile:]
        after = jnp.where(lax.broadcasted_iota(jnp.int32, (visit, depth), 0) == visit - 1, high, after)
        for tap, value in enumerate((before, full[tile:], after)):
            place = pl.ds(pl.multiple_of((slot * taps + tap) * depth, LANES), depth)
            xcat[1, pl.ds(kept, visit), place] = value.astype(BF16)
        return carry

    def build(k, slot):
        shard = shard_of(slot)
        cols = pl.ds(pl.multiple_of(shard * depth, LANES), depth)
        mid = embed[k, :, cols]
        wide_mid = mid.astype(F32)
        low = halo[k, 0, :, cols].astype(F32)[tile - 1 : tile]
        high = halo[k, 1, :, cols].astype(F32)[0:1]
        low = jnp.where(s == 0, 0.0, low)
        high = jnp.where(s == 3, 0.0, high)
        before = jnp.where(line == 0, low, pltpu.roll(wide_mid, 1, 0))
        after = jnp.where(line == rows - 1, high, pltpu.roll(wide_mid, rows - 1, 0))
        for tap, value in enumerate((before.astype(BF16), mid, after.astype(BF16))):
            xcat[k, :, pl.ds(pl.multiple_of((slot * taps + tap) * depth, LANES), depth)] = value

    def near(k, m):
        cols = pl.ds(pl.multiple_of(m * wide, wide), wide)
        own_rows = pl.ds(0, kept if k else rows)
        acc[k, own_rows, cols] = (
            jnp.dot(xcat[k, own_rows, pl.ds(0, half)], wbuf[m, pl.ds(0, half)], preferred_element_type=F32)
            + cb_ref[:, cols]
        )

    def remote_part(k, m):
        cols = pl.ds(pl.multiple_of(m * wide, wide), wide)
        own_rows = pl.ds(0, kept if k else rows)
        total = acc[k, own_rows, cols] + jnp.dot(
            xcat[k, own_rows, pl.ds(half, half)], wbuf[m, pl.ds(half, half)], preferred_element_type=F32
        )
        hidden = gelu(total).astype(BF16)
        logits[k, own_rows] = logits[k, own_rows] + jnp.dot(hidden, headw[cols, :], preferred_element_type=F32)

    def guest_part(m, carry):
        cols = pl.ds(pl.multiple_of(m * wide, wide), wide)
        part_rows = pl.ds(kept, visit)
        total = jnp.dot(xcat[1, part_rows, :], wbuf[m], preferred_element_type=F32) + cb_ref[:, cols]
        hidden = gelu(total).astype(BF16)
        logits[1, part_rows] = logits[1, part_rows] + jnp.dot(hidden, headw[cols, :], preferred_element_type=F32)
        return carry

    for copy in loads[:2]:
        copy.wait()
    for copy in halos:
        copy.wait()

    def first(i, carry):
        build(i % 2, i // 2)
        return carry

    lax.fori_loop(0, 4, first, 0)

    def step(j, carry):
        @pl.when(j < units)
        def _():
            x_copy(j).wait_recv()
            y_copy(cx, j).start()

            @pl.when(y == 0)
            def _():
                z_copy(cx, j).start()

            m_copy(0, cx, j).start()

        @pl.when((j >= LAG) & (j < units + LAG))
        def _():
            y_copy(cy, j - LAG).wait_recv()

            @pl.when(y == 1)
            def _():
                z_copy(cy, j - LAG).start()

            m_copy(1, cy, j - LAG).start()

        @pl.when((j >= 2 * LAG) & (j < units + 2 * LAG))
        def _():
            z_copy(cz, j - 2 * LAG).wait_recv()
            m_copy(2, cz, j - 2 * LAG).start()

        @pl.when(j == units - 2)
        def _():
            guests.start()

        @pl.when(j == 0)
        def _():
            lax.fori_loop(4, 8, first, 0)
            for copy in loads[2:]:
                copy.wait()
            for copy in own:
                copy.wait()

        pace = SPLIT // 2

        @pl.when((j >= 1) & ((j - 1) % pace == 0) & (j < units + 1))
        def _():
            i = (j - 1) // pace

            @pl.when(i % 2 == 0)
            def _():
                near(1, i // 2)

            @pl.when(i % 2 == 1)
            def _():
                near(0, i // 2)

        late = j - SPLIT - 2 * LAG

        @pl.when((late >= 0) & (late % pace == 0))
        def _():
            k = 1 - late // pace % 2
            m = late // SPLIT

            @pl.when(k == 1)
            def _():
                for kind, color in enumerate((cx, cy, cz)):
                    for u in range(SPLIT):
                        m_copy(kind, color, SPLIT * m + u).wait_recv()

                remote_part(1, m)

            @pl.when(k == 0)
            def _():
                remote_part(0, m)

        return carry

    lax.fori_loop(0, units + 2 * LAG + 1, step, 0)

    def t_copy(p):
        cols = pl.ds(p * wide, wide)
        return remote(sendt.at[pl.ds(0, kept), cols], rev_out.at[pl.ds(visit, kept), cols], t_send.at[p], t_recv.at[p], {"seq": mirror})

    for p in range(pieces):
        cols = pl.ds(p * wide, wide)
        value = softplus(logits[1, pl.ds(0, kept), cols]).astype(BF16)
        turn = flip[pl.ds(visit, kept), pl.ds(0, kept)]
        sendt[pl.ds(0, kept), cols] = jnp.dot(turn, value, preferred_element_type=F32).astype(BF16)
        if p:
            t_copy(p - 1).start()
    remote_part(0, blocks - 1)
    t_copy(pieces - 1).start()
    keep = []
    for p in range(pieces):
        cols = pl.ds(p * wide, wide)
        keept[:, cols] = softplus(logits[0, :, cols]).astype(BF16)
        keep.append(pltpu.make_async_copy(keept.at[:, cols], fwd_out.at[:, cols], out_sem.at[p]))
        if p:
            keep[p - 1].start()

    guests.wait_recv()
    keep[-1].start()
    lax.fori_loop(0, 4, build_guest, 0)
    lax.fori_loop(0, blocks, guest_part, 0)
    value = softplus(logits[1, pl.ds(kept, visit)]).astype(BF16)
    turn = flip[pl.ds(0, visit), pl.ds(kept, visit)]
    sendt[pl.ds(kept, visit)] = jnp.dot(turn, value, preferred_element_type=F32).astype(BF16)
    keep.append(pltpu.make_async_copy(sendt.at[pl.ds(kept, visit)], rev_out.at[pl.ds(0, visit)], out_sem.at[pieces]))

    def drain(j, carry):
        x_copy(j).wait_send()
        y_copy(cx, j).wait_send()
        z_copy(2 * z, j).wait_send()
        for kind, color in enumerate((cx, cy, cz)):
            m_copy(kind, color, j).wait_send()
        return carry

    lax.fori_loop(0, units, drain, 0)
    keep[-1].start()
    for copy in keep:
        copy.wait()
    guests.wait_send()
    for p in range(pieces):
        t_copy(p).wait()


def fused(forward_embed, reverse_embed, conv_weight, conv_bias, head_weight, head_bias):
    rows, channels = forward_embed.shape
    _, taps, depth, _ = conv_weight.shape
    tracks = head_weight.shape[1]
    blocks = channels // WIDE
    units = SPLIT * blocks
    pieces = tracks // WIDE
    dma = pltpu.SemaphoreType.DMA
    anywhere = pl.BlockSpec(memory_space=pl.ANY)
    vmem = pl.BlockSpec(memory_space=pltpu.VMEM)
    forward_tracks, reverse_tracks = pl.pallas_call(
        functools.partial(kernel, taps),
        out_shape=[jax.ShapeDtypeStruct((rows, tracks), BF16)] * 2,
        in_specs=[anywhere, anywhere, anywhere, vmem, anywhere, vmem],
        out_specs=[anywhere, anywhere],
        scratch_shapes=[
            pltpu.VMEM((2, rows, channels), BF16),
            pltpu.VMEM((2, 2, 16, channels), BF16),
            pltpu.VMEM((rows // 2 + 16, channels), BF16),
            pltpu.VMEM((2, rows, 4 * taps * depth), BF16),
            pltpu.VMEM((blocks, 4 * taps * depth, WIDE), BF16),
            pltpu.VMEM((2, rows, channels), F32),
            pltpu.VMEM((channels, tracks), BF16),
            pltpu.VMEM((2, rows, tracks), F32),
            pltpu.VMEM((rows, rows), BF16),
            pltpu.VMEM((rows, tracks), BF16),
            pltpu.VMEM((rows, tracks), BF16),
            dma((3 + taps * blocks,)),
            dma((2, 2)), dma((2, 2)),
            dma((taps, blocks)), dma((taps, blocks)),
            dma((units,)), dma((units,)),
            dma((units,)), dma((units,)),
            dma((units,)), dma((units,)),
            dma((3, units)), dma((3, units)),
            dma((pieces,)), dma((pieces,)), dma((pieces + 1,)), dma((2,)),
        ],
        compiler_params=pltpu.CompilerParams(
            collective_id=0, has_side_effects=True, vmem_limit_bytes=62 * 1024 * 1024
        ),
    )(forward_embed, reverse_embed, conv_weight, conv_bias, head_weight, head_bias[None])
    return (0.5 * (forward_tracks.astype(F32) + reverse_tracks.astype(F32))).astype(BF16)


def with_halo(block, axis):
    count = lax.axis_size(axis)
    forward = [(i, i + 1) for i in range(count - 1)]
    backward = [(target, source) for source, target in forward]
    low = lax.ppermute(block[-1:], axis, forward)
    high = lax.ppermute(block[:1], axis, backward)
    return jnp.concatenate([low, block, high], axis=0)


def general(forward_embed, reverse_embed, conv_weight, conv_bias, head_weight, head_bias):
    count = lax.axis_size("seq")
    layers, taps = conv_weight.shape[:2]
    gathered = [lax.all_gather(conv_weight[n], "seq", axis=1, tiled=True) for n in range(layers)]

    def strand(hidden):
        for n in range(layers):
            rows = hidden.shape[0]
            padded = with_halo(hidden, "seq")
            total = sum(
                jnp.dot(padded[k : k + rows], gathered[n][k], preferred_element_type=F32) for k in range(taps)
            )
            hidden = jax.nn.gelu(total + conv_bias[n], approximate=False).astype(BF16)
        logits = jnp.dot(hidden, head_weight, preferred_element_type=F32) + head_bias
        return jax.nn.softplus(logits).astype(BF16)

    reverse_tracks = strand(reverse_embed)[::-1]
    reverse_tracks = lax.ppermute(reverse_tracks, "seq", [(i, count - 1 - i) for i in range(count)])
    mean = 0.5 * (strand(forward_embed).astype(F32) + reverse_tracks.astype(F32))
    return mean.astype(BF16)


def solution(mesh):
    cubes = mesh.shape["seq"] == 4 and mesh.shape["batch"] % 4 == 0
    return jax.shard_map(
        fused if cubes else general,
        mesh=mesh,
        in_specs=(
            P(("batch", "seq"), None),
            P(("batch", "seq"), None),
            P(None, None, "seq", None),
            P(),
            P(),
            P(),
        ),
        out_specs=P(("batch", "seq"), None),
        check_vma=False,
    )
```
